256 devices in a mesh: slab: 8 (over z), region: 32 (over x, y, core).
Axes of the slice: x: 4, y: 4, z: 8, core: 2. Of those that a mesh axis runs over, the one named last changes fastest.
Arguments:
- prior_matrix: float32 [256, 524288], P('region', 'slab'), may hold values from -6 to 6
- prior_at_measurements: float32 [256, 16384], P('region', 'slab'), may hold values from -6 to 6
- scaled_residual_vector: float32 [256, 16384], P('region', 'slab'), may hold values from -6 to 6
- lattice_coordinates: float32 [2, 524288], P(None, 'slab'), may hold values from 0 to 2
- measurement_coordinates: float32 [2, 16384], replicated, may hold values from 0 to 2
- neighbour_block_totals: int32 [4096], P('slab'), may hold values from 2 to 16, as said below
- neighbour_block_numbers: int32 [4096, 16], P('slab'), may hold values from 0 to 19, as said below
Outputs:
- analysis: float32 [256, 524288], P('region', 'slab')
The draws below stay inside these ranges and needn't reach their ends.
Inputs may be any that keep to these rules, and one draw needn't show every extreme that they name: neighbour_block_totals[t] observation tiles are listed for grid tile t; in every slab some grid tile lists 16 and some lists 2. `neighbour_block_numbers`: row t's first neighbour_block_totals[t] entries are distinct, and each names an observation tile s * 16 - 2 + e that exists (from 0 to 16 * 8 - 1), s being t's slab; the remaining entries of the row are 0.
All inputs are finite; a program needn't handle non-finite values.
Results may differ from the reference program's by a relative error of at most 0.0003.
Values sent between devices are 32-bit elements; how exact they have to be, the bound alone decides.
No kernel may reach another device: no remote copies, remote signals or barrier semaphores. Data moves between devices by JAX's collectives and lax.ppermute only.
A program may use at most 64 MiB of HBM per device.

```python
import jax
import jax.numpy as jnp
from jax import lax

MEMBERSHIP_TOTAL = 256
BLOCK_NODES = 128
OBS_TILE = 128
TILES_REGION = 16
OBS_SLAB = 16
EDGE = 2
LIST_MOST = 16
TILES_SLAB = 512
GRID_TILES = 4096
LATTICE_NODES = 524288
MEASUREMENTS = 16384


def block_order(subkey):
    return jax.random.permutation(subkey, TILES_SLAB // TILES_REGION)


def counts_helper(key):
    base_key = jax.random.fold_in(key, 7)
    slabs = GRID_TILES // TILES_SLAB
    regions = TILES_SLAB // TILES_REGION
    dense_count = max(1, regions // 4)
    subkeys = jax.random.split(base_key, 3)
    block_rank = jax.vmap(block_order)(jax.random.split(subkeys[0], slabs))
    dense = block_rank < dense_count
    dense_tiles = jnp.repeat(dense, TILES_REGION, axis=1)
    high_draw = jax.random.randint(subkeys[1], (slabs, TILES_SLAB), LIST_MOST * 3 // 4, LIST_MOST + 1)
    low_draw = jax.random.randint(subkeys[2], (slabs, TILES_SLAB), 2, max(3, LIST_MOST // 2))
    counts = jnp.where(dense_tiles, high_draw, low_draw)
    counts = counts.at[:, 0].set(LIST_MOST)
    counts = counts.at[:, 1].set(2)
    return counts.reshape(GRID_TILES).astype(jnp.int32)


def draw_neighbour_block_totals(key, part):
    return counts_helper(key)


def draw_neighbour_block_numbers(key, part):
    counts = counts_helper(key)
    extended = OBS_SLAB + 2 * EDGE
    slabs = GRID_TILES // TILES_SLAB
    tile_slab = jnp.arange(GRID_TILES, dtype=jnp.int32) // TILES_SLAB
    ext_ids = jnp.arange(extended, dtype=jnp.int32)[None, :]
    global_tile = tile_slab[:, None] * OBS_SLAB - EDGE + ext_ids
    valid = (global_tile >= 0) & (global_tile < OBS_SLAB * slabs)
    scores = jax.random.randint(jax.random.fold_in(key, 11), (GRID_TILES, extended), 0, 1 << 16) * extended + ext_ids
    scores = jnp.where(valid, scores, scores + (1 << 26))
    picked = jnp.argsort(scores, axis=1)[:, :LIST_MOST].astype(jnp.int32)
    used = jnp.arange(LIST_MOST, dtype=jnp.int32)[None, :] < counts[:, None]
    return jnp.where(used, picked, 0).astype(jnp.int32)


def levels(rng, extent, cuts, smallest, largest):
    loudness, own = 1.0, jax.random.fold_in(rng, 6)
    for dim, blocks in cuts:
        heights = jnp.exp(jax.random.uniform(jax.random.fold_in(own, dim), (blocks,), jnp.float32, smallest / len(cuts), largest / len(cuts)))
        loudness = loudness * jnp.repeat(heights, extent[dim] // blocks).reshape([-1 if axis == dim else 1 for axis in range(len(extent))])
    return loudness


def normal_values(stream_key, dims, scale, bound, cuts=(), held_as=jnp.bfloat16):
    values = jax.random.normal(stream_key, dims, jnp.float32) * scale
    if len(cuts) > 0:
        values = levels(stream_key, dims, cuts, -0.22, 0.18) * values
    return jnp.clip(values, min=-bound, max=bound).astype(held_as)


def setup_inputs(seed: int = 0) -> dict:
    keys = jax.random.split(jax.random.key(seed), 8)
    prior_matrix = normal_values(keys[0], (MEMBERSHIP_TOTAL, LATTICE_NODES), 1.0, 6.0, ((0, 32), (1, 8)), jnp.float32)
    prior_at_measurements = normal_values(keys[1], (MEMBERSHIP_TOTAL, MEASUREMENTS), 1.0, 6.0, ((0, 32), (1, 8)), jnp.float32)
    scaled_residual_vector = normal_values(keys[2], (MEMBERSHIP_TOTAL, MEASUREMENTS), 1.0, 6.0, ((0, 32), (1, 8)), jnp.float32)
    lattice_coordinates = jnp.clip(2.0 * jax.random.uniform(keys[3], (2, LATTICE_NODES), jnp.float32) ** levels(keys[3], (2, LATTICE_NODES), ((1, 8),), -0.2, 0.2), 0.0, 2.0)
    measurement_coordinates = jnp.clip(jax.random.uniform(keys[4], (2, MEASUREMENTS), jnp.float32, 0.0, 2.0), 0.0, 2.0)
    neighbour_block_totals = draw_neighbour_block_totals(jax.random.fold_in(keys[7], 71), 0)
    neighbour_block_numbers = draw_neighbour_block_numbers(jax.random.fold_in(keys[7], 71), 0)
    return {"prior_matrix": prior_matrix, "prior_at_measurements": prior_at_measurements, "scaled_residual_vector": scaled_residual_vector, "lattice_coordinates": lattice_coordinates, "measurement_coordinates": measurement_coordinates, "neighbour_block_totals": neighbour_block_totals, "neighbour_block_numbers": neighbour_block_numbers}


exact_dot = lax.Precision.HIGHEST

def gaspari_cohn(scaled):
    near_part = scaled * scaled * (scaled * (scaled * (-0.25 * scaled + 0.5) + 0.625) - 5.0 / 3.0) + 1.0
    safe_scaled = jnp.maximum(scaled, 1.0)
    far_part = safe_scaled * (safe_scaled * (safe_scaled * (safe_scaled * (safe_scaled / 12.0 - 0.5) + 0.625) + 5.0 / 3.0) - 5.0) + 4.0 - 2.0 / (3.0 * safe_scaled)
    return jnp.where(scaled <= 1.0, near_part, jnp.where(scaled <= 2.0, far_part, jnp.zeros_like(scaled)))

def taper_tile(grid_xy, obs_xy):
    delta_x = grid_xy[0][:, None] - obs_xy[0][None, :]
    delta_y = grid_xy[1][:, None] - obs_xy[1][None, :]
    distance = jnp.sqrt(delta_x * delta_x + delta_y * delta_y)
    return gaspari_cohn(distance)

def pair_term(lattice_deviation, obs_tile, innov_tile, taper, realization_vectors):
    covariance = lax.dot_general(lattice_deviation, obs_tile, (((0,), (0,)), ((), ())), precision=exact_dot, preferred_element_type=jnp.float32) / (realization_vectors - 1.0)
    weighted = taper * covariance
    return lax.dot_general(innov_tile, weighted, (((1,), (1,)), ((), ())), precision=exact_dot, preferred_element_type=jnp.float32)

def reference(prior_matrix, prior_at_measurements, scaled_residual_vector, lattice_coordinates, measurement_coordinates, neighbour_block_totals, neighbour_block_numbers):
    realization_vectors = prior_matrix.shape[0]
    prior_deviation = prior_matrix - lax.optimization_barrier(jnp.mean(prior_matrix, axis=0, keepdims=True))
    measured_deviation = prior_at_measurements - lax.optimization_barrier(jnp.mean(prior_at_measurements, axis=0, keepdims=True))
    margin = EDGE * OBS_TILE
    padded_anom = jnp.pad(measured_deviation, ((0, 0), (margin, margin)))
    padded_innov = jnp.pad(scaled_residual_vector, ((0, 0), (margin, margin)))
    padded_xy = jnp.pad(measurement_coordinates, ((0, 0), (margin, margin)))

    def one_tile(tile_id):
        slab_index = tile_id // TILES_SLAB
        starting_node = tile_id * BLOCK_NODES
        lattice_deviation = lax.dynamic_slice_in_dim(prior_deviation, starting_node, BLOCK_NODES, 1)
        grid_xy = lax.dynamic_slice_in_dim(lattice_coordinates, starting_node, BLOCK_NODES, 1)

        def add_pair(position, summed):
            ext_id = neighbour_block_numbers[tile_id, position]
            column = ((slab_index * OBS_SLAB + ext_id) * OBS_TILE).astype(jnp.int32)
            obs_tile = lax.dynamic_slice_in_dim(padded_anom, column, OBS_TILE, 1)
            innov_tile = lax.dynamic_slice_in_dim(padded_innov, column, OBS_TILE, 1)
            obs_xy = lax.dynamic_slice_in_dim(padded_xy, column, OBS_TILE, 1)
            taper = taper_tile(grid_xy, obs_xy)
            return summed + pair_term(lattice_deviation, obs_tile, innov_tile, taper, realization_vectors)
        empty = jnp.zeros((realization_vectors, BLOCK_NODES), jnp.float32)
        return lax.fori_loop(0, neighbour_block_totals[tile_id], add_pair, empty)
    increments = lax.map(one_tile, jnp.arange(GRID_TILES, dtype=jnp.int32))
    posterior_correction = jnp.transpose(increments, (1, 0, 2)).reshape(realization_vectors, GRID_TILES * BLOCK_NODES)
    return prior_matrix + posterior_correction
```

```python
import functools

import jax
import jax.numpy as jnp
from jax import lax
from jax.experimental import pallas as pl
from jax.experimental.pallas import tpu as pltpu
from jax.sharding import PartitionSpec as P

BLOCK_NODES = 128
OBS_TILE = 128
OBS_SLAB = 16
EDGE = 2
OBS_EXT = OBS_SLAB + 2 * EDGE
RING = 4
OFFSETS = (0, -1, 1, 2)


def region_shift(block, dx, dy, dc):
    pairs = []
    for source in range(RING * RING * 2):
        x, y, c = source // 8, (source // 2) % 4, source % 2
        pairs.append((source, ((x + dx) % 4) * 8 + ((y + dy) % 4) * 2 + (c ^ dc)))
    return lax.ppermute(block, "region", pairs)


def gather_ring(block, dx, dy):
    return jnp.concatenate(
        [
            block,
            region_shift(block, dx, dy, 0),
            region_shift(block, -dx, -dy, 0),
            region_shift(block, 2 * dx, 2 * dy, 0),
        ],
        axis=0,
    )


def pack_kernel(me, order, totals, listed, tiles, packed, plan):
    def copy(p, carry):
        packed[p] = tiles[order[p]]
        return carry

    lax.fori_loop(0, packed.shape[0], copy, 0, unroll=16)
    tiles_all = order.shape[0]
    slots = tiles_all // 32

    def tile_plan(slot, count):
        tile = order[me[0] * slots + slot]
        total = totals[tile]

        def group(g, count):
            second = 2 * g + 1
            q0 = listed[2 * g * tiles_all + tile]
            q1 = listed[jnp.minimum(second, total - 1) * tiles_all + tile]
            plan[count] = slot
            plan[128 + count] = q0
            plan[256 + count] = q1
            plan[384 + count] = jnp.where(second < total, 1, 0)
            return count + 1

        return lax.fori_loop(0, lax.div(total + 1, 2), group, count)

    count = lax.fori_loop(0, slots, tile_plan, 0)
    plan[512] = count


def taper_of(dx, dy):
    square = jnp.maximum(dx * dx + dy * dy, 1e-30)
    inverse = lax.rsqrt(square)
    z = square * inverse
    near = square * (z * (z * (-0.25 * z + 0.5) + 0.625) - 5.0 / 3.0) + 1.0
    far = (
        z * (z * (z * (z * (z * (1.0 / 12.0) - 0.5) + 0.625) + 5.0 / 3.0) - 5.0)
        + 4.0
        - (2.0 / 3.0) * inverse
    )
    return jnp.where(z <= 1.0, near, jnp.where(z <= 2.0, far, 0.0))


def halves(value):
    high = value.astype(jnp.bfloat16)
    low = (value - high.astype(jnp.float32)).astype(jnp.bfloat16)
    return high, low


def analysis_kernel(
    plan, order_a, order_b, mine, recv, obs, obs_other, inn, inn_other, lattice, obs_xy,
    out, obs3, inn_high, inn_low, anom3, total, weights, place_x, place_y,
):
    members = 256
    slots = recv.shape[1]

    def prepare_obs(q, carry):
        whole = jnp.concatenate(
            [obs[:, q].reshape(members // 2, OBS_TILE), obs_other[:, q].reshape(members // 2, OBS_TILE)],
            axis=0,
        )
        anom = (whole - jnp.mean(whole, axis=0, keepdims=True)) * (1.0 / (members - 1.0))
        high, low = halves(anom.T)
        obs3[q, :, 0:members] = high
        obs3[q, :, members : 2 * members] = high
        obs3[q, :, 2 * members : 3 * members] = low
        whole = jnp.concatenate(
            [inn[:, q].reshape(members // 2, OBS_TILE), inn_other[:, q].reshape(members // 2, OBS_TILE)],
            axis=0,
        )
        high, low = halves(whole)
        inn_high[q] = high
        inn_low[q] = low
        xy = obs_xy[q]
        place_x[q] = jnp.broadcast_to(xy[0:1], (OBS_TILE, OBS_TILE)).T
        place_y[q] = jnp.broadcast_to(xy[1:2], (OBS_TILE, OBS_TILE)).T
        return carry

    lax.fori_loop(0, OBS_EXT, prepare_obs, 0)

    def prepare_tile(slot, carry):
        rows = jnp.concatenate([recv[order_a[b], slot] for b in range(32)], axis=0)
        high, low = halves(rows - jnp.mean(rows, axis=0, keepdims=True))
        anom3[slot, 0:members] = high
        anom3[slot, members : 2 * members] = low
        anom3[slot, 2 * members : 3 * members] = high
        for b in range(32):
            total[slot, 8 * b : 8 * b + 8] = recv[order_b[b], slot]
        return carry

    lax.fori_loop(0, slots, prepare_tile, 0)
    weights[...] = jnp.zeros_like(weights)
    count = plan[512]

    def step(i, carry):
        before = jnp.maximum(i - 1, 0)
        b_slot, b0, b1 = plan[before], plan[128 + before], plan[256 + before]
        left = jnp.concatenate(
            [inn_high[b0], inn_high[b1], inn_low[b0], inn_low[b1], inn_high[b0], inn_high[b1]], axis=1
        )
        total[b_slot] += jnp.dot(left, weights[...], preferred_element_type=jnp.float32)

        now = jnp.minimum(i, count - 1)
        slot, q0, q1, keep = plan[now], plan[128 + now], plan[256 + now], plan[384 + now]
        cov = jnp.dot(
            jnp.concatenate([obs3[q0], obs3[q1]], axis=0),
            anom3[slot],
            preferred_element_type=jnp.float32,
        )
        grid_xy = lattice[mine[slot]]
        grid_x, grid_y = grid_xy[0:1], grid_xy[1:2]
        first = taper_of(grid_x - place_x[q0], grid_y - place_y[q0]) * cov[:OBS_TILE]
        other = taper_of(grid_x - place_x[q1], grid_y - place_y[q1]) * cov[OBS_TILE:]
        other = other * keep.astype(jnp.float32)
        high, low = halves(jnp.concatenate([first, other], axis=0))
        weights[0:256] = high
        weights[256:512] = high
        weights[512:768] = low
        return carry

    lax.fori_loop(0, count + 1, step, 0)

    def put(slot, carry):
        for b in range(32):
            out[order_b[b], slot] = total[slot, 8 * b : 8 * b + 8]
        return carry

    lax.fori_loop(0, slots, put, 0)


def unpack_kernel(order, received, out):
    def copy(p, carry):
        out[order[p]] = received[p]
        return carry

    lax.fori_loop(0, received.shape[0], copy, 0, unroll=16)


VMEM = pl.BlockSpec(memory_space=pltpu.VMEM)
SMEM = pl.BlockSpec(memory_space=pltpu.SMEM)


def per_device(
    prior_matrix,
    prior_at_measurements,
    scaled_residual_vector,
    lattice_coordinates,
    measurement_coordinates,
    neighbour_block_totals,
    neighbour_block_numbers,
):
    regions = lax.axis_size("region")
    slabs = lax.axis_size("slab")
    region = lax.axis_index("region")
    slab = lax.axis_index("slab")
    tiles = neighbour_block_totals.shape[0]
    slots = tiles // regions

    both = jnp.stack((prior_at_measurements, scaled_residual_vector))
    margin = EDGE * OBS_TILE
    up = [(i, i + 1) for i in range(slabs - 1)]
    low = lax.ppermute(both[:, :, -margin:], "slab", up)
    high = lax.ppermute(both[:, :, :margin], "slab", [(t, s) for s, t in up])

    index = jnp.arange(tiles, dtype=jnp.int32)
    key = neighbour_block_totals * tiles + (tiles - 1 - index)
    rank = jnp.sum((key[None, :] > key[:, None]).astype(jnp.int32), axis=1)
    row, col = rank // regions, rank % regions
    where_to = jnp.where(row % 2 == 0, col, regions - 1 - col) * slots + row
    order = jnp.sum(jnp.where(where_to[None, :] == index[:, None], index[None, :], 0), axis=1)

    packed, plan = pl.pallas_call(
        pack_kernel,
        out_shape=(
            jax.ShapeDtypeStruct((tiles, 8, BLOCK_NODES), jnp.float32),
            jax.ShapeDtypeStruct((640,), jnp.int32),
        ),
        in_specs=[SMEM, SMEM, SMEM, SMEM, VMEM],
        out_specs=(VMEM, SMEM),
        name="pack",
    )(
        region.reshape(1),
        order,
        neighbour_block_totals,
        neighbour_block_numbers.T.reshape(-1),
        prior_matrix.reshape(8, tiles, BLOCK_NODES).transpose(1, 0, 2),
    )
    received = lax.all_to_all(packed, "region", split_axis=0, concat_axis=0, tiled=True)

    wide = jnp.concatenate([low, both, high], axis=2)
    wide = wide.reshape(2, 8, OBS_EXT, OBS_TILE).transpose(0, 2, 1, 3)
    obs, inn = gather_ring(wide[0], 1, 0), gather_ring(wide[1], 0, 1)
    obs, inn = gather_ring(obs, 0, 1), gather_ring(inn, 1, 0)
    obs_other, inn_other = region_shift(obs, 0, 0, 1), region_shift(inn, 0, 0, 1)
    shape = (RING * RING, OBS_EXT, 8, OBS_TILE)

    x, y, c = region // 8, (region // 2) % 4, region % 2
    offsets = jnp.array(OFFSETS, jnp.int32)
    xs, ys, cs = (x + offsets) % 4, (y + offsets) % 4, jnp.stack((c, 1 - c))
    order_a = (cs[:, None, None] + 2 * ys[None, :, None] + 8 * xs[None, None, :]).reshape(-1)
    order_b = (cs[:, None, None] + 8 * xs[None, :, None] + 2 * ys[None, None, :]).reshape(-1)

    padded_xy = jnp.pad(measurement_coordinates, ((0, 0), (margin, margin)))
    ext_xy = lax.dynamic_slice_in_dim(padded_xy, slab * OBS_SLAB * OBS_TILE, OBS_EXT * OBS_TILE, 1)
    ext_xy = ext_xy.reshape(2, OBS_EXT, OBS_TILE).transpose(1, 0, 2)
    mine = lax.dynamic_slice_in_dim(order, region * slots, slots)

    analysis = pl.pallas_call(
        analysis_kernel,
        out_shape=jax.ShapeDtypeStruct((regions, slots, 8, BLOCK_NODES), jnp.float32),
        in_specs=[SMEM] * 4 + [VMEM] * 7,
        out_specs=VMEM,
        scratch_shapes=[
            pltpu.VMEM((OBS_EXT, OBS_TILE, 768), jnp.bfloat16),
            pltpu.VMEM((OBS_EXT, 256, OBS_TILE), jnp.bfloat16),
            pltpu.VMEM((OBS_EXT, 256, OBS_TILE), jnp.bfloat16),
            pltpu.VMEM((slots, 768, BLOCK_NODES), jnp.bfloat16),
            pltpu.VMEM((slots, 256, BLOCK_NODES), jnp.float32),
            pltpu.VMEM((768, BLOCK_NODES), jnp.bfloat16),
            pltpu.VMEM((OBS_EXT, OBS_TILE, BLOCK_NODES), jnp.float32),
            pltpu.VMEM((OBS_EXT, OBS_TILE, BLOCK_NODES), jnp.float32),
        ],
        name="analysis",
    )(
        plan,
        order_a,
        order_b,
        mine,
        received.reshape(regions, slots, 8, BLOCK_NODES),
        obs.reshape(shape),
        obs_other.reshape(shape),
        inn.reshape(shape),
        inn_other.reshape(shape),
        lattice_coordinates.reshape(2, tiles, BLOCK_NODES).transpose(1, 0, 2),
        ext_xy,
    )
    returned = lax.all_to_all(
        analysis.reshape(tiles, 8, BLOCK_NODES), "region", split_axis=0, concat_axis=0, tiled=True
    )
    out = pl.pallas_call(
        unpack_kernel,
        out_shape=jax.ShapeDtypeStruct((tiles, 8, BLOCK_NODES), jnp.float32),
        in_specs=[SMEM, VMEM],
        out_specs=VMEM,
        name="unpack",
    )(order, returned)
    return out.transpose(1, 0, 2).reshape(8, tiles * BLOCK_NODES)


def solution(mesh):
    in_specs = (
        P("region", "slab"),
        P("region", "slab"),
        P("region", "slab"),
        P(None, "slab"),
        P(),
        P("slab"),
        P("slab", None),
    )
    return jax.shard_map(
        per_device, mesh=mesh, in_specs=in_specs, out_specs=P("region", "slab"), check_vma=False
    )
```

```python
import functools

import functools

import jax
import jax.numpy as jnp
from jax import lax
from jax.experimental import pallas as pl
from jax.experimental.pallas import tpu as pltpu
from jax.sharding import PartitionSpec as P


BLOCK_NODES = 128
OBS_TILE = 128
OBS_SLAB = 16
EDGE = 2
OBS_EXT = OBS_SLAB + 2 * EDGE
RING = 4
OFFSETS = (0, -1, 1, 2)
DEPTH = 6


def region_shift(block, dx, dy, dc):
    pairs = []
    for source in range(RING * RING * 2):
        x, y, c = source // 8, (source // 2) % 4, source % 2
        pairs.append((source, ((x + dx) % 4) * 8 + ((y + dy) % 4) * 2 + (c ^ dc)))
    return lax.ppermute(block, "region", pairs)


def ring_pieces(block, dx, dy):
    return [
        block,
        region_shift(block, dx, dy, 0),
        region_shift(block, -dx, -dy, 0),
        region_shift(block, 2 * dx, 2 * dy, 0),
    ]


COUNT, ORDER_A, ORDER_B, MINE = 512, 544, 576, 608


def pack_kernel(me, order, totals, listed, tiles, packed, plan):
    def copy(p, carry):
        packed[p] = tiles[order[p]]
        return carry

    lax.fori_loop(0, packed.shape[0], copy, 0, unroll=16)
    region = me[0]
    slots = order.shape[0] // 32

    def tile_plan(slot, count):
        tile = order[region * slots + slot]
        plan[MINE + slot] = tile
        total = totals[tile]

        def group(g, count):
            second = 2 * g + 1
            plan[count] = slot
            plan[128 + count] = listed[2 * g, tile]
            plan[256 + count] = listed[jnp.minimum(second, total - 1), tile]
            plan[384 + count] = jnp.where(second < total, 2, 1)
            return count + 1

        return lax.fori_loop(0, lax.div(total + 1, 2), group, count)

    plan[COUNT] = 0
    count = 0
    for half in range(2):
        count = lax.fori_loop(half * slots // 2, (half + 1) * slots // 2, tile_plan, count)
        odd = count & 1

        @pl.when(odd == 1)
        def _(count=count, half=half):
            plan[count] = (half + 1) * slots // 2 - 1
            plan[128 + count] = plan[128 + count - 1]
            plan[256 + count] = plan[256 + count - 1]
            plan[384 + count] = 0

        count = count + odd
        plan[COUNT + 1 + half] = count

    x, y, c = lax.shift_right_logical(region, 3), lax.shift_right_logical(region, 1) & 3, region & 1
    for b in range(32):
        core = (c + b // 16) & 1
        outer, inner = OFFSETS[(b // 4) % 4], OFFSETS[b % 4]
        plan[ORDER_A + b] = ((x + inner) & 3) * 8 + ((y + outer) & 3) * 2 + core
        plan[ORDER_B + b] = ((x + outer) & 3) * 8 + ((y + inner) & 3) * 2 + core


def taper_of(dx, dy):
    square = jnp.maximum(dx * dx + dy * dy, 1e-30)
    inverse = lax.rsqrt(square)
    z = square * inverse
    near = square * (z * (z * (-0.25 * z + 0.5) + 0.625) - 5.0 / 3.0) + 1.0
    far = (
        z * (z * (z * (z * (z * (1.0 / 12.0) - 0.5) + 0.625) + 5.0 / 3.0) - 5.0)
        + 4.0
        - (2.0 / 3.0) * inverse
    )
    return jnp.where(z <= 1.0, near, jnp.where(z <= 2.0, far, 0.0))


def halves(value):
    high = value.astype(jnp.bfloat16)
    low = (value - high.astype(jnp.float32)).astype(jnp.bfloat16)
    return high, low


def taper_kernel(me, plan, lattice, obs_xy, tapers, place_x, place_y, held, sent):
    count = plan[COUNT + 2]
    depth = held.shape[0]

    def place(q, carry):
        tile = me[1] * OBS_SLAB - EDGE + q
        xy = obs_xy[jnp.minimum(jnp.maximum(tile, 0), obs_xy.shape[0] - 1)]
        place_x[q] = jnp.broadcast_to(xy[0:1], (OBS_TILE, OBS_TILE)).T
        place_y[q] = jnp.broadcast_to(xy[1:2], (OBS_TILE, OBS_TILE)).T
        return carry

    lax.fori_loop(0, OBS_EXT, place, 0)

    def out_copy(i):
        k = lax.rem(i, depth)
        return pltpu.make_async_copy(held.at[k], tapers.at[i], sent.at[k])

    def group(i, carry):
        @pl.when(i >= depth)
        def _():
            out_copy(i - depth).wait()

        slot, q0, q1, keep = plan[i], plan[128 + i], plan[256 + i], plan[384 + i]
        grid_xy = lattice[plan[MINE + slot]]
        grid_x, grid_y = grid_xy[0:1], grid_xy[1:2]
        k = lax.rem(i, depth)
        first = taper_of(grid_x - place_x[q0], grid_y - place_y[q0])
        held[k, :OBS_TILE] = first * jnp.minimum(keep, 1).astype(jnp.float32)
        other = taper_of(grid_x - place_x[q1], grid_y - place_y[q1])
        held[k, OBS_TILE:] = other * jnp.maximum(keep - 1, 0).astype(jnp.float32)
        out_copy(i).start()
        return carry

    lax.fori_loop(0, count, group, 0)

    def drain(i, carry):
        out_copy(i).wait()
        return carry

    lax.fori_loop(jnp.maximum(count - depth, 0), count, drain, 0)


def split_kernel(*refs):
    members = 256
    obs, inn, (obs_out, inn_out) = refs[: 2 * RING], refs[2 * RING : 4 * RING], refs[4 * RING :]

    def rows(pieces, q):
        return jnp.concatenate([p[:, q].reshape(8 * RING, OBS_TILE) for p in pieces], axis=0)

    for q in range(obs[0].shape[1]):
        whole = rows(obs, q)
        anom = (whole - jnp.mean(whole, axis=0, keepdims=True)) * (1.0 / (members - 1.0))
        high, low = halves(anom.T)
        obs_out[q, :OBS_TILE] = high
        obs_out[q, OBS_TILE:] = low
        high, low = halves(rows(inn, q))
        inn_out[q, :members] = high
        inn_out[q, members:] = low


def analysis_kernel(
    half, plan, recv, obs_any, inn_any, tapers, out,
    obs, inn, anom, total, weights, held, arrived, loaded,
):
    members = 256
    slots = recv.shape[1]
    start = plan[COUNT + half]
    count = plan[COUNT + half + 1]
    depth = held.shape[0]

    obs_copy = pltpu.make_async_copy(obs_any, obs, loaded.at[0])
    inn_copy = pltpu.make_async_copy(inn_any, inn, loaded.at[1])
    obs_copy.start()
    inn_copy.start()

    def in_copy(i):
        k = lax.rem(i, depth)
        return pltpu.make_async_copy(tapers.at[i], held.at[k], arrived.at[k])

    def first_copy(i, carry):
        in_copy(i).start()
        return carry

    lax.fori_loop(start, jnp.minimum(count, start + depth - 2), first_copy, 0)

    def prepare_tile(slot, carry):
        rows = jnp.concatenate([recv[plan[ORDER_A + b], slot] for b in range(32)], axis=0)
        high, low = halves(rows - jnp.mean(rows, axis=0, keepdims=True))
        anom[slot, :, :BLOCK_NODES] = high
        anom[slot, :, BLOCK_NODES:] = low
        for b in range(32):
            total[slot, 8 * b : 8 * b + 8] = recv[plan[ORDER_B + b], slot]
        return carry

    lax.fori_loop(0, slots, prepare_tile, 0)
    weights[...] = jnp.zeros_like(weights)
    obs_copy.wait()
    inn_copy.wait()

    def add_group(i, k):
        slot, q0, q1 = plan[i] - half * slots, plan[128 + i], plan[256 + i]
        left = jnp.concatenate([inn[q0], inn[q1]], axis=1)
        both = jnp.dot(left, weights[k], preferred_element_type=jnp.float32)
        total[slot] += (
            both[:members, :BLOCK_NODES] + both[:members, BLOCK_NODES:] + both[members:, :BLOCK_NODES]
        )

    def weigh_group(i):
        slot = plan[i] - half * slots
        left = jnp.concatenate([obs[plan[128 + i]], obs[plan[256 + i]]], axis=0)
        both = jnp.dot(left, anom[slot], preferred_element_type=jnp.float32)
        parts = []
        for j in (0, 2 * OBS_TILE):
            top, low = both[j : j + OBS_TILE], both[j + OBS_TILE : j + 2 * OBS_TILE]
            parts.append(top[:, :BLOCK_NODES] + top[:, BLOCK_NODES:] + low[:, :BLOCK_NODES])
        return halves(held[lax.rem(i, depth)] * jnp.concatenate(parts, axis=0))

    def step(n, carry):
        i = start + 2 * n
        for k in range(2):
            @pl.when(i + k + depth - 2 < count)
            def _(k=k):
                in_copy(i + k + depth - 2).start()

        for k in range(2):
            in_copy(i + k).wait()
        before = jnp.maximum(i - 2, start)
        for k in range(2):
            add_group(before + k, k)
        for k in range(2):
            high, low = weigh_group(i + k)
            weights[k, :, :BLOCK_NODES] = high
            weights[k, :, BLOCK_NODES:] = low
        return carry

    lax.fori_loop(0, lax.div(count - start, 2), step, 0)
    for k in range(2):
        add_group(count - 2 + k, k)

    def put(slot, carry):
        for b in range(32):
            out[plan[ORDER_B + b], slot] = total[slot, 8 * b : 8 * b + 8]
        return carry

    lax.fori_loop(0, slots, put, 0)


def unpack_kernel(order, first, second, out):
    slots = first.shape[1]

    def copy(device, carry):
        for half, received in enumerate((first, second)):
            for j in range(slots):
                out[order[(2 * device + half) * slots + j]] = received[device, j]
        return carry

    lax.fori_loop(0, first.shape[0], copy, 0)


VMEM = pl.BlockSpec(memory_space=pltpu.VMEM)
SMEM = pl.BlockSpec(memory_space=pltpu.SMEM)
ANY = pl.BlockSpec(memory_space=pl.ANY)


def per_device(
    prior_matrix,
    prior_at_measurements,
    scaled_residual_vector,
    lattice_coordinates,
    measurement_coordinates,
    neighbour_block_totals,
    neighbour_block_numbers,
):
    regions = lax.axis_size("region")
    slabs = lax.axis_size("slab")
    region = lax.axis_index("region")
    slab = lax.axis_index("slab")
    tiles = neighbour_block_totals.shape[0]
    slots = tiles // regions

    me = jnp.stack((region, slab))

    both = jnp.stack((prior_at_measurements, scaled_residual_vector))
    margin = EDGE * OBS_TILE
    up = [(i, i + 1) for i in range(slabs - 1)]
    low = lax.ppermute(both[:, :, -margin:], "slab", up)
    high = lax.ppermute(both[:, :, :margin], "slab", [(t, s) for s, t in up])

    index = jnp.arange(tiles, dtype=jnp.int32)
    key = neighbour_block_totals * tiles + (tiles - 1 - index)
    rank = jnp.sum((key[None, :] > key[:, None]).astype(jnp.int32), axis=1)
    row, col = rank // regions, rank % regions
    where_to = jnp.where(row % 2 == 0, col, regions - 1 - col) * slots + row
    order = jnp.sum(jnp.where(where_to[None, :] == index[:, None], index[None, :], 0), axis=1)

    packed, plan = pl.pallas_call(
        pack_kernel,
        out_shape=(
            jax.ShapeDtypeStruct((tiles, 8, BLOCK_NODES), jnp.float32),
            jax.ShapeDtypeStruct((640,), jnp.int32),
        ),
        in_specs=[SMEM, SMEM, SMEM, SMEM, VMEM],
        out_specs=(VMEM, SMEM),
        name="pack",
    )(
        me,
        order,
        neighbour_block_totals,
        neighbour_block_numbers.T,
        prior_matrix.reshape(8, tiles, BLOCK_NODES).transpose(1, 0, 2),
    )
    received = lax.all_to_all(packed, "region", split_axis=0, concat_axis=0, tiled=True)

    wide = jnp.concatenate([low, both, high], axis=2)
    wide = wide.reshape(2, 8, OBS_EXT, OBS_TILE).transpose(0, 2, 1, 3)
    obs = jnp.concatenate(ring_pieces(wide[0], 1, 0), axis=0)
    inn = jnp.concatenate(ring_pieces(wide[1], 0, 1), axis=0)
    obs, inn = ring_pieces(obs, 0, 1), ring_pieces(inn, 1, 0)
    obs_other, inn_other = [region_shift(obs[0], 0, 0, 1)], [region_shift(inn[0], 0, 0, 1)]
    for k in range(1, RING):
        obs_other.append(region_shift(obs[k], 0, 0, 1))
        inn_other.append(region_shift(inn[k], 0, 0, 1))
    gathered = [p.reshape(RING, OBS_EXT, 8, OBS_TILE) for p in obs + obs_other + inn + inn_other]

    tapers = pl.pallas_call(
        taper_kernel,
        out_shape=jax.ShapeDtypeStruct((128, 2 * OBS_TILE, BLOCK_NODES), jnp.float32),
        in_specs=[SMEM, SMEM, VMEM, VMEM],
        out_specs=ANY,
        scratch_shapes=[
            pltpu.VMEM((OBS_EXT, OBS_TILE, BLOCK_NODES), jnp.float32),
            pltpu.VMEM((OBS_EXT, OBS_TILE, BLOCK_NODES), jnp.float32),
            pltpu.VMEM((DEPTH, 2 * OBS_TILE, BLOCK_NODES), jnp.float32),
            pltpu.SemaphoreType.DMA((DEPTH,)),
        ],
        cost_estimate=pl.CostEstimate(flops=10**10, bytes_accessed=8 * 2**20, transcendentals=0),
        name="taper",
    )(
        me,
        plan,
        lattice_coordinates.reshape(2, tiles, BLOCK_NODES).transpose(1, 0, 2),
        measurement_coordinates.reshape(2, -1, OBS_TILE).transpose(1, 0, 2),
    )

    part = OBS_EXT // 4
    obs_split, inn_split = pl.pallas_call(
        split_kernel,
        grid=(4,),
        out_shape=(
            jax.ShapeDtypeStruct((OBS_EXT, 2 * OBS_TILE, 256), jnp.bfloat16),
            jax.ShapeDtypeStruct((OBS_EXT, 512, OBS_TILE), jnp.bfloat16),
        ),
        in_specs=[pl.BlockSpec((RING, part, 8, OBS_TILE), lambda i: (0, i, 0, 0))] * 16,
        out_specs=(
            pl.BlockSpec((part, 2 * OBS_TILE, 256), lambda i: (i, 0, 0)),
            pl.BlockSpec((part, 512, OBS_TILE), lambda i: (i, 0, 0)),
        ),
        cost_estimate=pl.CostEstimate(flops=5 * 10**9, bytes_accessed=10 * 2**20, transcendentals=0),
        name="split",
    )(*gathered)

    some = slots // 2
    returned = []
    for half in range(2):
        analysis = pl.pallas_call(
            functools.partial(analysis_kernel, half),
            grid=(1,),
            out_shape=jax.ShapeDtypeStruct((regions, some, 8, BLOCK_NODES), jnp.float32),
            in_specs=[
                SMEM,
                pl.BlockSpec((regions, some, 8, BLOCK_NODES), lambda i, half=half: (0, half, 0, 0)),
                ANY,
                ANY,
                ANY,
            ],
            out_specs=pl.BlockSpec((regions, some, 8, BLOCK_NODES), lambda i: (0, 0, 0, 0)),
            scratch_shapes=[
                pltpu.VMEM((OBS_EXT, 2 * OBS_TILE, 256), jnp.bfloat16),
                pltpu.VMEM((OBS_EXT, 512, OBS_TILE), jnp.bfloat16),
                pltpu.VMEM((some, 256, 2 * BLOCK_NODES), jnp.bfloat16),
                pltpu.VMEM((some, 256, BLOCK_NODES), jnp.float32),
                pltpu.VMEM((2, 256, 2 * BLOCK_NODES), jnp.bfloat16),
                pltpu.VMEM((DEPTH, 2 * OBS_TILE, BLOCK_NODES), jnp.float32),
                pltpu.SemaphoreType.DMA((DEPTH,)),
                pltpu.SemaphoreType.DMA((2,)),
            ],
            cost_estimate=pl.CostEstimate(flops=10**10, bytes_accessed=8 * 2**20, transcendentals=0),
        )(plan, received.reshape(regions, slots, 8, BLOCK_NODES), obs_split, inn_split, tapers)
        returned.append(lax.all_to_all(analysis, "region", split_axis=0, concat_axis=0, tiled=True))
    out = pl.pallas_call(
        unpack_kernel,
        out_shape=jax.ShapeDtypeStruct((tiles, 8, BLOCK_NODES), jnp.float32),
        in_specs=[SMEM, VMEM, VMEM],
        out_specs=VMEM,
        name="unpack",
    )(order, *returned)
    return out.transpose(1, 0, 2).reshape(8, tiles * BLOCK_NODES)


def solution(mesh):
    in_specs = (
        P("region", "slab"),
        P("region", "slab"),
        P("region", "slab"),
        P(None, "slab"),
        P(),
        P("slab"),
        P("slab", None),
    )

    return jax.shard_map(
        per_device, mesh=mesh, in_specs=in_specs, out_specs=P("region", "slab"), check_vma=False
    )
```

```python
import functools

import jax
import jax.numpy as jnp
from jax import lax
from jax.experimental import pallas as pl
from jax.experimental.pallas import tpu as pltpu
from jax.sharding import PartitionSpec as P


BLOCK_NODES = 128
OBS_TILE = 128
OBS_SLAB = 16
EDGE = 2
OBS_EXT = OBS_SLAB + 2 * EDGE
RING = 4
OFFSETS = (0, -1, 1, 2)
DEPTH = 6


def region_shift(block, dx, dy, dc):
    pairs = []
    for source in range(RING * RING * 2):
        x, y, c = source // 8, (source // 2) % 4, source % 2
        pairs.append((source, ((x + dx) % 4) * 8 + ((y + dy) % 4) * 2 + (c ^ dc)))
    return lax.ppermute(block, "region", pairs)


def ring_pieces(block, dx, dy):
    return [
        block,
        region_shift(block, dx, dy, 0),
        region_shift(block, -dx, -dy, 0),
        region_shift(block, 2 * dx, 2 * dy, 0),
    ]


COUNT, ORDER_A, ORDER_B, MINE = 512, 544, 576, 608


def pack_kernel(me, order, totals, listed, tiles, packed, plan):
    def copy(p, carry):
        packed[p] = tiles[order[p]]
        return carry

    lax.fori_loop(0, packed.shape[0], copy, 0, unroll=16)
    region = me[0]
    slots = order.shape[0] // 32

    def tile_plan(slot, count):
        tile = order[region * slots + slot]
        plan[MINE + slot] = tile
        total = totals[tile]

        def group(g, count):
            second = 2 * g + 1
            plan[count] = slot
            plan[128 + count] = listed[2 * g, tile]
            plan[256 + count] = listed[jnp.minimum(second, total - 1), tile]
            plan[384 + count] = jnp.where(second < total, 2, 1)
            return count + 1

        return lax.fori_loop(0, lax.div(total + 1, 2), group, count)

    count = lax.fori_loop(0, slots, tile_plan, 0)

    @pl.when(count & 1 == 1)
    def _():
        plan[count] = slots - 1
        plan[128 + count] = plan[128 + count - 1]
        plan[256 + count] = plan[256 + count - 1]
        plan[384 + count] = 0

    plan[COUNT] = count + (count & 1)
    x, y, c = lax.shift_right_logical(region, 3), lax.shift_right_logical(region, 1) & 3, region & 1
    for b in range(32):
        core = (c + b // 16) & 1
        outer, inner = OFFSETS[(b // 4) % 4], OFFSETS[b % 4]
        plan[ORDER_A + b] = ((x + inner) & 3) * 8 + ((y + outer) & 3) * 2 + core
        plan[ORDER_B + b] = ((x + outer) & 3) * 8 + ((y + inner) & 3) * 2 + core


def taper_of(dx, dy):
    square = jnp.maximum(dx * dx + dy * dy, 1e-30)
    inverse = lax.rsqrt(square)
    z = square * inverse
    near = square * (z * (z * (-0.25 * z + 0.5) + 0.625) - 5.0 / 3.0) + 1.0
    beyond = jnp.maximum(z - 1.0, 0.0)
    twice = beyond * beyond
    value = near + (twice * twice) * (beyond * ((2.0 / 3.0) * inverse + 1.0 / 3.0))
    return jnp.where(z <= 2.0, value, 0.0)


def halves(value):
    high = value.astype(jnp.bfloat16)
    low = (value - high.astype(jnp.float32)).astype(jnp.bfloat16)
    return high, low


def taper_kernel(half, me, plan, lattice, obs_xy, *refs):
    tapers, place_x, place_y, held, sent = refs[-5:]
    count = plan[COUNT]
    middle = lax.div(count * 2, 3)
    start, stop = ((0, middle), (middle, count))[half]
    depth = held.shape[0]

    def place(q, carry):
        tile = me[1] * OBS_SLAB - EDGE + q
        xy = obs_xy[jnp.minimum(jnp.maximum(tile, 0), obs_xy.shape[0] - 1)]
        place_x[q] = jnp.broadcast_to(xy[0:1], (OBS_TILE, OBS_TILE)).T
        place_y[q] = jnp.broadcast_to(xy[1:2], (OBS_TILE, OBS_TILE)).T
        return carry

    lax.fori_loop(0, OBS_EXT, place, 0)

    def out_copy(i):
        k = lax.rem(i, depth)
        return pltpu.make_async_copy(held.at[k], tapers.at[i], sent.at[k])

    def group(i, carry):
        @pl.when(i >= start + depth)
        def _():
            out_copy(i - depth).wait()

        slot, q0, q1, keep = plan[i], plan[128 + i], plan[256 + i], plan[384 + i]
        grid_xy = lattice[plan[MINE + slot]]
        grid_x, grid_y = grid_xy[0:1], grid_xy[1:2]
        k = lax.rem(i, depth)
        for j, q in enumerate((q0, q1)):
            away = grid_x + jnp.where(keep > j, 0.0, 16.0)
            rows = pl.ds(j * OBS_TILE, OBS_TILE)
            held[k, rows] = taper_of(away - place_x[q], grid_y - place_y[q])
        out_copy(i).start()
        return carry

    lax.fori_loop(start, stop, group, 0)

    def drain(i, carry):
        out_copy(i).wait()
        return carry

    lax.fori_loop(jnp.maximum(stop - depth, start), stop, drain, 0)


def split_kernel(*refs):
    members = 256
    pieces, (obs_out, inn_out, whole, obs, inn, here, gone) = refs[: 4 * RING], refs[4 * RING :]
    loads = []
    for k, piece in enumerate(pieces):
        place = whole.at[k // (2 * RING), k % (2 * RING)]
        loads.append(pltpu.make_async_copy(piece, place, here.at[k]))
    for load in loads:
        load.start()
    for load in loads:
        load.wait()

    def stores(q):
        return (
            pltpu.make_async_copy(obs.at[q], obs_out.at[q], gone.at[0, q]),
            pltpu.make_async_copy(inn.at[q], inn_out.at[q], gone.at[1, q]),
        )

    def tile(q, carry):
        value = whole[0, :, :, q].reshape(members, OBS_TILE)
        anom = (value - jnp.mean(value, axis=0, keepdims=True)) * (1.0 / (members - 1.0))
        high, low = halves(anom.T)
        obs[q, :OBS_TILE] = high
        obs[q, OBS_TILE:] = low
        high, low = halves(whole[1, :, :, q].reshape(members, OBS_TILE))
        inn[q, :members] = high
        inn[q, members:] = low
        for store in stores(q):
            store.start()
        return carry

    lax.fori_loop(0, OBS_EXT, tile, 0)

    def drain(q, carry):
        for store in stores(q):
            store.wait()
        return carry

    lax.fori_loop(0, OBS_EXT, drain, 0)


def analysis_kernel(
    plan, recv_any, obs_any, inn_any, tapers, out,
    recv, obs, inn, anom, total, weights, held, arrived, loaded,
):
    members = 256
    slots = recv.shape[1]
    count = plan[COUNT]
    depth = held.shape[0]

    recv_copy = pltpu.make_async_copy(recv_any, recv, loaded.at[0])
    obs_copy = pltpu.make_async_copy(obs_any, obs, loaded.at[1])
    inn_copy = pltpu.make_async_copy(inn_any, inn, loaded.at[2])
    for copy in (recv_copy, obs_copy, inn_copy):
        copy.start()

    def in_copy(i):
        k = lax.rem(i, depth)
        return pltpu.make_async_copy(tapers.at[i], held.at[k], arrived.at[k])

    def first_copy(i, carry):
        in_copy(i).start()
        return carry

    lax.fori_loop(0, jnp.minimum(count, depth - 2), first_copy, 0)

    def prepare_tile(slot, carry):
        rows = jnp.concatenate([recv[plan[ORDER_A + b], slot] for b in range(32)], axis=0)
        high, low = halves(rows - jnp.mean(rows, axis=0, keepdims=True))
        anom[slot, :, :BLOCK_NODES] = high
        anom[slot, :, BLOCK_NODES:] = low
        for b in range(32):
            total[slot, 8 * b : 8 * b + 8] = recv[plan[ORDER_B + b], slot]
        return carry

    recv_copy.wait()
    lax.fori_loop(0, slots, prepare_tile, 0)
    weights[...] = jnp.zeros_like(weights)
    obs_copy.wait()
    inn_copy.wait()

    def add_group(i, k):
        slot, q0, q1 = plan[i], plan[128 + i], plan[256 + i]
        left = jnp.concatenate([inn[q0], inn[q1]], axis=1)
        both = jnp.dot(left, weights[k], preferred_element_type=jnp.float32)
        total[slot] += (
            both[:members, :BLOCK_NODES] + both[:members, BLOCK_NODES:] + both[members:, :BLOCK_NODES]
        )

    def weigh_group(i):
        slot = plan[i]
        left = jnp.concatenate([obs[plan[128 + i]], obs[plan[256 + i]]], axis=0)
        both = jnp.dot(left, anom[slot], preferred_element_type=jnp.float32)
        parts = []
        for j in (0, 2 * OBS_TILE):
            top, low = both[j : j + OBS_TILE], both[j + OBS_TILE : j + 2 * OBS_TILE]
            parts.append(top[:, :BLOCK_NODES] + top[:, BLOCK_NODES:] + low[:, :BLOCK_NODES])
        return halves(held[lax.rem(i, depth)] * jnp.concatenate(parts, axis=0))

    def step(n, carry):
        i = 2 * n
        for k in range(2):
            @pl.when(i + k + depth - 2 < count)
            def _(k=k):
                in_copy(i + k + depth - 2).start()

        for k in range(2):
            in_copy(i + k).wait()
        before = jnp.maximum(i - 2, 0)
        for k in range(2):
            add_group(before + k, k)
        for k in range(2):
            high, low = weigh_group(i + k)
            weights[k, :, :BLOCK_NODES] = high
            weights[k, :, BLOCK_NODES:] = low
        return carry

    lax.fori_loop(0, lax.div(count, 2), step, 0)
    for k in range(2):
        add_group(count - 2 + k, k)

    def put(slot, carry):
        for b in range(32):
            out[plan[ORDER_B + b], slot] = total[slot, 8 * b : 8 * b + 8]
        return carry

    lax.fori_loop(0, slots, put, 0)


def unpack_kernel(order, received, out):
    def copy(p, carry):
        out[order[p]] = received[p]
        return carry

    lax.fori_loop(0, received.shape[0], copy, 0, unroll=16)


VMEM = pl.BlockSpec(memory_space=pltpu.VMEM)
SMEM = pl.BlockSpec(memory_space=pltpu.SMEM)
ANY = pl.BlockSpec(memory_space=pl.ANY)


def per_device(
    prior_matrix,
    prior_at_measurements,
    scaled_residual_vector,
    lattice_coordinates,
    measurement_coordinates,
    neighbour_block_totals,
    neighbour_block_numbers,
):
    regions = lax.axis_size("region")
    slabs = lax.axis_size("slab")
    region = lax.axis_index("region")
    slab = lax.axis_index("slab")
    tiles = neighbour_block_totals.shape[0]
    slots = tiles // regions

    me = jnp.stack((region, slab))

    both = jnp.stack((prior_at_measurements, scaled_residual_vector))
    margin = EDGE * OBS_TILE
    up = [(i, i + 1) for i in range(slabs - 1)]
    low = lax.ppermute(both[:, :, -margin:], "slab", up)
    high = lax.ppermute(both[:, :, :margin], "slab", [(t, s) for s, t in up])

    index = jnp.arange(tiles, dtype=jnp.int32)
    key = neighbour_block_totals * tiles + (tiles - 1 - index)
    rank = jnp.sum((key[None, :] > key[:, None]).astype(jnp.int32), axis=1)
    row, col = rank // regions, rank % regions
    where_to = jnp.where(row % 2 == 0, col, regions - 1 - col) * slots + (slots - 1 - row)
    order = jnp.sum(jnp.where(where_to[None, :] == index[:, None], index[None, :], 0), axis=1)

    packed, plan = pl.pallas_call(
        pack_kernel,
        out_shape=(
            jax.ShapeDtypeStruct((tiles, 8, BLOCK_NODES), jnp.float32),
            jax.ShapeDtypeStruct((640,), jnp.int32),
        ),
        in_specs=[SMEM, SMEM, SMEM, SMEM, VMEM],
        out_specs=(VMEM, SMEM),
        name="pack",
    )(
        me,
        order,
        neighbour_block_totals,
        neighbour_block_numbers.T,
        prior_matrix.reshape(8, tiles, BLOCK_NODES).transpose(1, 0, 2),
    )
    received = lax.all_to_all(packed, "region", split_axis=0, concat_axis=0, tiled=True)

    wide = jnp.concatenate([low, both, high], axis=2)
    wide = wide.reshape(2, 8, OBS_EXT, OBS_TILE).transpose(0, 2, 1, 3)
    obs = jnp.concatenate(ring_pieces(wide[0], 1, 0), axis=0)
    inn = jnp.concatenate(ring_pieces(wide[1], 0, 1), axis=0)
    obs, inn = ring_pieces(obs, 0, 1), ring_pieces(inn, 1, 0)
    obs_other, inn_other = [region_shift(obs[0], 0, 0, 1)], [region_shift(inn[0], 0, 0, 1)]
    for k in range(1, RING):
        obs_other.append(region_shift(obs[k], 0, 0, 1))
        inn_other.append(region_shift(inn[k], 0, 0, 1))
    gathered = [p.reshape(RING, OBS_EXT, 8, OBS_TILE) for p in obs + obs_other + inn + inn_other]

    tapers = []
    for half in range(2):
        tapers = [
            pl.pallas_call(
                functools.partial(taper_kernel, half),
                out_shape=jax.ShapeDtypeStruct((128, 2 * OBS_TILE, BLOCK_NODES), jnp.float32),
                in_specs=[SMEM, SMEM, VMEM, VMEM] + [ANY] * len(tapers),
                out_specs=ANY,
                scratch_shapes=[
                    pltpu.VMEM((OBS_EXT, OBS_TILE, BLOCK_NODES), jnp.float32),
                    pltpu.VMEM((OBS_EXT, OBS_TILE, BLOCK_NODES), jnp.float32),
                    pltpu.VMEM((DEPTH, 2 * OBS_TILE, BLOCK_NODES), jnp.float32),
                    pltpu.SemaphoreType.DMA((DEPTH,)),
                ],
                input_output_aliases={4: 0} if tapers else {},
                cost_estimate=pl.CostEstimate(
                    flops=5 * 10**9, bytes_accessed=4 * 2**20, transcendentals=0
                ),
            )(
                me,
                plan,
                lattice_coordinates.reshape(2, tiles, BLOCK_NODES).transpose(1, 0, 2),
                measurement_coordinates.reshape(2, -1, OBS_TILE).transpose(1, 0, 2),
                *tapers,
            )
        ]

    obs_split, inn_split = pl.pallas_call(
        split_kernel,
        out_shape=(
            jax.ShapeDtypeStruct((OBS_EXT, 2 * OBS_TILE, 256), jnp.bfloat16),
            jax.ShapeDtypeStruct((OBS_EXT, 512, OBS_TILE), jnp.bfloat16),
        ),
        in_specs=[ANY] * (4 * RING),
        out_specs=(ANY, ANY),
        scratch_shapes=[
            pltpu.VMEM((2, 2 * RING, RING, OBS_EXT, 8, OBS_TILE), jnp.float32),
            pltpu.VMEM((OBS_EXT, 2 * OBS_TILE, 256), jnp.bfloat16),
            pltpu.VMEM((OBS_EXT, 512, OBS_TILE), jnp.bfloat16),
            pltpu.SemaphoreType.DMA((4 * RING,)),
            pltpu.SemaphoreType.DMA((2, OBS_EXT)),
        ],
        cost_estimate=pl.CostEstimate(flops=5 * 10**9, bytes_accessed=10 * 2**20, transcendentals=0),
        name="split",
    )(*gathered)

    analysis = pl.pallas_call(
        analysis_kernel,
        out_shape=jax.ShapeDtypeStruct((regions, slots, 8, BLOCK_NODES), jnp.float32),
        in_specs=[SMEM] + [ANY] * 4,
        out_specs=VMEM,
        scratch_shapes=[
            pltpu.VMEM((regions, slots, 8, BLOCK_NODES), jnp.float32),
            pltpu.VMEM((OBS_EXT, 2 * OBS_TILE, 256), jnp.bfloat16),
            pltpu.VMEM((OBS_EXT, 512, OBS_TILE), jnp.bfloat16),
            pltpu.VMEM((slots, 256, 2 * BLOCK_NODES), jnp.bfloat16),
            pltpu.VMEM((slots, 256, BLOCK_NODES), jnp.float32),
            pltpu.VMEM((2, 256, 2 * BLOCK_NODES), jnp.bfloat16),
            pltpu.VMEM((DEPTH, 2 * OBS_TILE, BLOCK_NODES), jnp.float32),
            pltpu.SemaphoreType.DMA((DEPTH,)),
            pltpu.SemaphoreType.DMA((3,)),
        ],
        cost_estimate=pl.CostEstimate(flops=2 * 10**10, bytes_accessed=16 * 2**20, transcendentals=0),
        name="analysis",
    )(plan, received.reshape(regions, slots, 8, BLOCK_NODES), obs_split, inn_split, tapers[0])
    returned = lax.all_to_all(
        analysis.reshape(tiles, 8, BLOCK_NODES), "region", split_axis=0, concat_axis=0, tiled=True
    )
    out = pl.pallas_call(
        unpack_kernel,
        out_shape=jax.ShapeDtypeStruct((tiles, 8, BLOCK_NODES), jnp.float32),
        in_specs=[SMEM, VMEM],
        out_specs=VMEM,
        name="unpack",
    )(order, returned)
    return out.transpose(1, 0, 2).reshape(8, tiles * BLOCK_NODES)


def solution(mesh):
    in_specs = (
        P("region", "slab"),
        P("region", "slab"),
        P("region", "slab"),
        P(None, "slab"),
        P(),
        P("slab"),
        P("slab", None),
    )

    return jax.shard_map(
        per_device, mesh=mesh, in_specs=in_specs, out_specs=P("region", "slab"), check_vma=False
    )
```

```python
import functools

import jax
import jax.numpy as jnp
from jax import lax
from jax.experimental import pallas as pl
from jax.experimental.pallas import tpu as pltpu
from jax.sharding import PartitionSpec as P


BLOCK_NODES = 128
OBS_TILE = 128
OBS_SLAB = 16
EDGE = 2
OBS_EXT = OBS_SLAB + 2 * EDGE
RING = 4
OFFSETS = (0, -1, 1, 2)
DEPTH = 6


def region_shift(block, dx, dy, dc):
    pairs = []
    for source in range(RING * RING * 2):
        x, y, c = source // 8, (source // 2) % 4, source % 2
        pairs.append((source, ((x + dx) % 4) * 8 + ((y + dy) % 4) * 2 + (c ^ dc)))
    return lax.ppermute(block, "region", pairs)


def ring_pieces(block, dx, dy):
    return [
        block,
        region_shift(block, dx, dy, 0),
        region_shift(block, -dx, -dy, 0),
        region_shift(block, 2 * dx, 2 * dy, 0),
    ]


GROUPS = 144
COUNT, ORDER_A, ORDER_B, MINE = 576, 592, 624, 656


def pack_kernel(me, order, totals, listed, tiles, packed, plan):
    def copy(p, carry):
        packed[p] = tiles[order[p]]
        return carry

    lax.fori_loop(0, packed.shape[0], copy, 0, unroll=16)
    region = me[0]
    slots = order.shape[0] // 32

    def tile_plan(slot, count):
        tile = order[region * slots + slot]
        plan[MINE + slot] = tile
        total = totals[tile]
        for g in range(listed.shape[0] // 2):
            plan[count + g] = slot
            plan[GROUPS + count + g] = listed[2 * g, tile]
            plan[2 * GROUPS + count + g] = listed[2 * g + 1, tile]
            plan[3 * GROUPS + count + g] = jnp.where(2 * g + 1 < total, 2, 1)
        return count + lax.div(total + 1, 2)

    count = lax.fori_loop(0, slots, tile_plan, 0)

    @pl.when(count & 1 == 1)
    def _():
        plan[count] = slots - 1
        plan[GROUPS + count] = plan[GROUPS + count - 1]
        plan[2 * GROUPS + count] = plan[2 * GROUPS + count - 1]
        plan[3 * GROUPS + count] = 0

    plan[COUNT] = count + (count & 1)
    x, y, c = lax.shift_right_logical(region, 3), lax.shift_right_logical(region, 1) & 3, region & 1
    for b in range(32):
        core = (c + b // 16) & 1
        outer, inner = OFFSETS[(b // 4) % 4], OFFSETS[b % 4]
        plan[ORDER_A + b] = ((x + inner) & 3) * 8 + ((y + outer) & 3) * 2 + core
        plan[ORDER_B + b] = ((x + outer) & 3) * 8 + ((y + inner) & 3) * 2 + core


def taper_of(dx, dy):
    square = jnp.maximum(dx * dx + dy * dy, 1e-30)
    inverse = lax.rsqrt(square)
    z = square * inverse
    near = square * (z * (z * (-0.25 * z + 0.5) + 0.625) - 5.0 / 3.0) + 1.0
    beyond = jnp.maximum(z - 1.0, 0.0)
    twice = beyond * beyond
    value = near + (twice * twice) * (beyond * ((2.0 / 3.0) * inverse + 1.0 / 3.0))
    return jnp.where(z <= 2.0, value, 0.0)


def halves(value):
    high = value.astype(jnp.bfloat16)
    low = (value - high.astype(jnp.float32)).astype(jnp.bfloat16)
    return high, low


def taper_kernel(half, me, plan, lattice, obs_xy, *refs):
    tapers, place_x, place_y, held, sent = refs[-5:]
    count = plan[COUNT]
    middle = lax.div(count * 2, 3)
    start, stop = ((0, middle), (middle, count))[half]
    depth = held.shape[0]

    def place(q, carry):
        tile = me[1] * OBS_SLAB - EDGE + q
        xy = obs_xy[jnp.minimum(jnp.maximum(tile, 0), obs_xy.shape[0] - 1)]
        place_x[q] = jnp.broadcast_to(xy[0:1], (OBS_TILE, OBS_TILE)).T
        place_y[q] = jnp.broadcast_to(xy[1:2], (OBS_TILE, OBS_TILE)).T
        return carry

    lax.fori_loop(0, OBS_EXT, place, 0)

    def out_copy(i):
        k = lax.rem(i, depth)
        return pltpu.make_async_copy(held.at[k], tapers.at[i], sent.at[k])

    def group(i, carry):
        @pl.when(i >= start + depth)
        def _():
            out_copy(i - depth).wait()

        slot, q0, q1, keep = plan[i], plan[GROUPS + i], plan[2 * GROUPS + i], plan[3 * GROUPS + i]
        grid_xy = lattice[plan[MINE + slot]]
        grid_x, grid_y = grid_xy[0:1], grid_xy[1:2]
        k = lax.rem(i, depth)
        for j, q in enumerate((q0, q1)):
            away = grid_x + jnp.where(keep > j, 0.0, 16.0)
            rows = pl.ds(j * OBS_TILE, OBS_TILE)
            held[k, rows] = taper_of(away - place_x[q], grid_y - place_y[q])
        out_copy(i).start()
        return carry

    lax.fori_loop(start, stop, group, 0)

    def drain(i, carry):
        out_copy(i).wait()
        return carry

    lax.fori_loop(jnp.maximum(stop - depth, start), stop, drain, 0)


def split_kernel(*refs):
    members = 256
    pieces, (obs_out, inn_out, whole, obs, inn, here, gone) = refs[: 4 * RING], refs[4 * RING :]
    loads = []
    for k, piece in enumerate(pieces):
        place = whole.at[k // (2 * RING), k % (2 * RING)]
        loads.append(pltpu.make_async_copy(piece, place, here.at[k]))
    for load in loads:
        load.start()
    for load in loads:
        load.wait()

    def stores(q):
        return (
            pltpu.make_async_copy(obs.at[q], obs_out.at[q], gone.at[0, q]),
            pltpu.make_async_copy(inn.at[q], inn_out.at[q], gone.at[1, q]),
        )

    def tile(q, carry):
        value = whole[0, :, :, q].reshape(members, OBS_TILE)
        anom = (value - jnp.mean(value, axis=0, keepdims=True)) * (1.0 / (members - 1.0))
        high, low = halves(anom.T)
        obs[q, :OBS_TILE] = high
        obs[q, OBS_TILE:] = low
        high, low = halves(whole[1, :, :, q].reshape(members, OBS_TILE))
        inn[q, :members] = high
        inn[q, members:] = low
        for store in stores(q):
            store.start()
        return carry

    lax.fori_loop(0, OBS_EXT, tile, 0)

    def drain(q, carry):
        for store in stores(q):
            store.wait()
        return carry

    lax.fori_loop(0, OBS_EXT, drain, 0)


def analysis_kernel(
    plan, recv_any, obs_any, inn_any, tapers, out,
    recv, obs, inn, anom, total, weights, held, arrived, loaded,
):
    members = 256
    slots = recv.shape[1]
    count = plan[COUNT]
    depth = held.shape[0]

    recv_copy = pltpu.make_async_copy(recv_any, recv, loaded.at[0])
    obs_copy = pltpu.make_async_copy(obs_any, obs, loaded.at[1])
    inn_copy = pltpu.make_async_copy(inn_any, inn, loaded.at[2])
    for copy in (recv_copy, obs_copy, inn_copy):
        copy.start()

    def in_copy(i):
        k = lax.rem(i, depth)
        return pltpu.make_async_copy(tapers.at[i], held.at[k], arrived.at[k])

    def first_copy(i, carry):
        in_copy(i).start()
        return carry

    lax.fori_loop(0, jnp.minimum(count, depth - 2), first_copy, 0)

    def prepare_tile(slot, carry):
        rows = jnp.concatenate([recv[plan[ORDER_A + b], slot] for b in range(32)], axis=0)
        high, low = halves(rows - jnp.mean(rows, axis=0, keepdims=True))
        anom[slot, :, :BLOCK_NODES] = high
        anom[slot, :, BLOCK_NODES:] = low
        for b in range(32):
            total[slot, 8 * b : 8 * b + 8] = recv[plan[ORDER_B + b], slot]
        return carry

    recv_copy.wait()
    lax.fori_loop(0, slots, prepare_tile, 0)
    weights[...] = jnp.zeros_like(weights)
    obs_copy.wait()
    inn_copy.wait()

    def add_group(i, k):
        slot, q0, q1 = plan[i], plan[GROUPS + i], plan[2 * GROUPS + i]
        left = jnp.concatenate([inn[q0], inn[q1]], axis=1)
        both = jnp.dot(left, weights[k], preferred_element_type=jnp.float32)
        total[slot] += (
            both[:members, :BLOCK_NODES] + both[:members, BLOCK_NODES:] + both[members:, :BLOCK_NODES]
        )

    def weigh_group(i):
        slot = plan[i]
        left = jnp.concatenate([obs[plan[GROUPS + i]], obs[plan[2 * GROUPS + i]]], axis=0)
        both = jnp.dot(left, anom[slot], preferred_element_type=jnp.float32)
        parts = []
        for j in (0, 2 * OBS_TILE):
            top, low = both[j : j + OBS_TILE], both[j + OBS_TILE : j + 2 * OBS_TILE]
            parts.append(top[:, :BLOCK_NODES] + top[:, BLOCK_NODES:] + low[:, :BLOCK_NODES])
        return halves(held[lax.rem(i, depth)] * jnp.concatenate(parts, axis=0))

    def step(n, carry):
        i = 2 * n
        for k in range(2):
            @pl.when(i + k + depth - 2 < count)
            def _(k=k):
                in_copy(i + k + depth - 2).start()

        for k in range(2):
            in_copy(i + k).wait()
        before = jnp.maximum(i - 2, 0)
        for k in range(2):
            add_group(before + k, k)
        for k in range(2):
            high, low = weigh_group(i + k)
            weights[k, :, :BLOCK_NODES] = high
            weights[k, :, BLOCK_NODES:] = low
        return carry

    lax.fori_loop(0, lax.div(count, 2), step, 0)
    for k in range(2):
        add_group(count - 2 + k, k)

    def put(slot, carry):
        for b in range(32):
            out[plan[ORDER_B + b], slot] = total[slot, 8 * b : 8 * b + 8]
        return carry

    lax.fori_loop(0, slots, put, 0)


def unpack_kernel(order, received, out):
    def copy(p, carry):
        out[order[p]] = received[p]
        return carry

    lax.fori_loop(0, received.shape[0], copy, 0, unroll=16)


VMEM = pl.BlockSpec(memory_space=pltpu.VMEM)
SMEM = pl.BlockSpec(memory_space=pltpu.SMEM)
ANY = pl.BlockSpec(memory_space=pl.ANY)


def per_device(
    prior_matrix,
    prior_at_measurements,
    scaled_residual_vector,
    lattice_coordinates,
    measurement_coordinates,
    neighbour_block_totals,
    neighbour_block_numbers,
):
    regions = lax.axis_size("region")
    slabs = lax.axis_size("slab")
    region = lax.axis_index("region")
    slab = lax.axis_index("slab")
    tiles = neighbour_block_totals.shape[0]
    slots = tiles // regions

    me = jnp.stack((region, slab))

    both = jnp.stack((prior_at_measurements, scaled_residual_vector))
    margin = EDGE * OBS_TILE
    up = [(i, i + 1) for i in range(slabs - 1)]
    low = lax.ppermute(both[:, :, -margin:], "slab", up)
    high = lax.ppermute(both[:, :, :margin], "slab", [(t, s) for s, t in up])

    index = jnp.arange(tiles, dtype=jnp.int32)
    key = neighbour_block_totals * tiles + (tiles - 1 - index)
    rank = jnp.sum((key[None, :] > key[:, None]).astype(jnp.int32), axis=1)
    row, col = rank // regions, rank % regions
    where_to = jnp.where(row % 2 == 0, col, regions - 1 - col) * slots + (slots - 1 - row)
    order = jnp.sum(jnp.where(where_to[None, :] == index[:, None], index[None, :], 0), axis=1)

    packed, plan = pl.pallas_call(
        pack_kernel,
        out_shape=(
            jax.ShapeDtypeStruct((tiles, 8, BLOCK_NODES), jnp.float32),
            jax.ShapeDtypeStruct((768,), jnp.int32),
        ),
        in_specs=[SMEM, SMEM, SMEM, SMEM, VMEM],
        out_specs=(VMEM, SMEM),
        name="pack",
    )(
        me,
        order,
        neighbour_block_totals,
        neighbour_block_numbers.T,
        prior_matrix.reshape(8, tiles, BLOCK_NODES).transpose(1, 0, 2),
    )
    received = lax.all_to_all(packed, "region", split_axis=0, concat_axis=0, tiled=True)

    wide = jnp.concatenate([low, both, high], axis=2)
    wide = wide.reshape(2, 8, OBS_EXT, OBS_TILE).transpose(0, 2, 1, 3)
    obs = jnp.concatenate(ring_pieces(wide[0], 1, 0), axis=0)
    inn = jnp.concatenate(ring_pieces(wide[1], 0, 1), axis=0)
    obs, inn = ring_pieces(obs, 0, 1), ring_pieces(inn, 1, 0)
    obs_other, inn_other = [region_shift(obs[0], 0, 0, 1)], [region_shift(inn[0], 0, 0, 1)]
    for k in range(1, RING):
        obs_other.append(region_shift(obs[k], 0, 0, 1))
        inn_other.append(region_shift(inn[k], 0, 0, 1))
    gathered = [p.reshape(RING, OBS_EXT, 8, OBS_TILE) for p in obs + obs_other + inn + inn_other]

    tapers = []
    for half in range(2):
        tapers = [
            pl.pallas_call(
                functools.partial(taper_kernel, half),
                out_shape=jax.ShapeDtypeStruct((128, 2 * OBS_TILE, BLOCK_NODES), jnp.float32),
                in_specs=[SMEM, SMEM, VMEM, VMEM] + [ANY] * len(tapers),
                out_specs=ANY,
                scratch_shapes=[
                    pltpu.VMEM((OBS_EXT, OBS_TILE, BLOCK_NODES), jnp.float32),
                    pltpu.VMEM((OBS_EXT, OBS_TILE, BLOCK_NODES), jnp.float32),
                    pltpu.VMEM((DEPTH, 2 * OBS_TILE, BLOCK_NODES), jnp.float32),
                    pltpu.SemaphoreType.DMA((DEPTH,)),
                ],
                input_output_aliases={4: 0} if tapers else {},
                cost_estimate=pl.CostEstimate(
                    flops=5 * 10**9, bytes_accessed=4 * 2**20, transcendentals=0
                ),
            )(
                me,
                plan,
                lattice_coordinates.reshape(2, tiles, BLOCK_NODES).transpose(1, 0, 2),
                measurement_coordinates.reshape(2, -1, OBS_TILE).transpose(1, 0, 2),
                *tapers,
            )
        ]

    obs_split, inn_split = pl.pallas_call(
        split_kernel,
        out_shape=(
            jax.ShapeDtypeStruct((OBS_EXT, 2 * OBS_TILE, 256), jnp.bfloat16),
            jax.ShapeDtypeStruct((OBS_EXT, 512, OBS_TILE), jnp.bfloat16),
        ),
        in_specs=[ANY] * (4 * RING),
        out_specs=(ANY, ANY),
        scratch_shapes=[
            pltpu.VMEM((2, 2 * RING, RING, OBS_EXT, 8, OBS_TILE), jnp.float32),
            pltpu.VMEM((OBS_EXT, 2 * OBS_TILE, 256), jnp.bfloat16),
            pltpu.VMEM((OBS_EXT, 512, OBS_TILE), jnp.bfloat16),
            pltpu.SemaphoreType.DMA((4 * RING,)),
            pltpu.SemaphoreType.DMA((2, OBS_EXT)),
        ],
        cost_estimate=pl.CostEstimate(flops=5 * 10**9, bytes_accessed=10 * 2**20, transcendentals=0),
        name="split",
    )(*gathered)

    analysis = pl.pallas_call(
        analysis_kernel,
        out_shape=jax.ShapeDtypeStruct((regions, slots, 8, BLOCK_NODES), jnp.float32),
        in_specs=[SMEM] + [ANY] * 4,
        out_specs=VMEM,
        scratch_shapes=[
            pltpu.VMEM((regions, slots, 8, BLOCK_NODES), jnp.float32),
            pltpu.VMEM((OBS_EXT, 2 * OBS_TILE, 256), jnp.bfloat16),
            pltpu.VMEM((OBS_EXT, 512, OBS_TILE), jnp.bfloat16),
            pltpu.VMEM((slots, 256, 2 * BLOCK_NODES), jnp.bfloat16),
            pltpu.VMEM((slots, 256, BLOCK_NODES), jnp.float32),
            pltpu.VMEM((2, 256, 2 * BLOCK_NODES), jnp.bfloat16),
            pltpu.VMEM((DEPTH, 2 * OBS_TILE, BLOCK_NODES), jnp.float32),
            pltpu.SemaphoreType.DMA((DEPTH,)),
            pltpu.SemaphoreType.DMA((3,)),
        ],
        cost_estimate=pl.CostEstimate(flops=2 * 10**10, bytes_accessed=16 * 2**20, transcendentals=0),
        name="analysis",
    )(plan, received.reshape(regions, slots, 8, BLOCK_NODES), obs_split, inn_split, tapers[0])
    returned = lax.all_to_all(
        analysis.reshape(tiles, 8, BLOCK_NODES), "region", split_axis=0, concat_axis=0, tiled=True
    )
    out = pl.pallas_call(
        unpack_kernel,
        out_shape=jax.ShapeDtypeStruct((tiles, 8, BLOCK_NODES), jnp.float32),
        in_specs=[SMEM, VMEM],
        out_specs=VMEM,
        name="unpack",
    )(order, returned)
    return out.transpose(1, 0, 2).reshape(8, tiles * BLOCK_NODES)


def solution(mesh):
    in_specs = (
        P("region", "slab"),
        P("region", "slab"),
        P("region", "slab"),
        P(None, "slab"),
        P(),
        P("slab"),
        P("slab", None),
    )

    return jax.shard_map(
        per_device, mesh=mesh, in_specs=in_specs, out_specs=P("region", "slab"), check_vma=False
    )
```

```python
import functools

import jax
import jax.numpy as jnp
from jax import lax
from jax.experimental import pallas as pl
from jax.experimental.pallas import tpu as pltpu
from jax.sharding import PartitionSpec as P


BLOCK_NODES = 128
OBS_TILE = 128
OBS_SLAB = 16
EDGE = 2
OBS_EXT = OBS_SLAB + 2 * EDGE
RING = 4
OFFSETS = (0, -1, 1, 2)
DEPTH = 6


def region_shift(block, dx, dy, dc):
    pairs = []
    for source in range(RING * RING * 2):
        x, y, c = source // 8, (source // 2) % 4, source % 2
        pairs.append((source, ((x + dx) % 4) * 8 + ((y + dy) % 4) * 2 + (c ^ dc)))
    return lax.ppermute(block, "region", pairs)


def ring_pieces(block, dx, dy):
    return [
        block,
        region_shift(block, dx, dy, 0),
        region_shift(block, -dx, -dy, 0),
        region_shift(block, 2 * dx, 2 * dy, 0),
    ]


GROUPS = 144
COUNT, ORDER_A, ORDER_B, MINE = 576, 592, 624, 656


def pack_kernel(me, order, totals, listed, tiles, packed, plan):
    def copy(p, carry):
        packed[p] = tiles[order[p]]
        return carry

    lax.fori_loop(0, packed.shape[0], copy, 0, unroll=64)
    region = me[0]
    slots = order.shape[0] // 32

    def tile_plan(slot, count):
        tile = order[region * slots + slot]
        plan[MINE + slot] = tile
        total = totals[tile]
        for g in range(listed.shape[0] // 2):
            plan[count + g] = slot
            plan[GROUPS + count + g] = listed[2 * g, tile]
            plan[2 * GROUPS + count + g] = listed[2 * g + 1, tile]
            plan[3 * GROUPS + count + g] = jnp.where(2 * g + 1 < total, 2, 1)
        return count + lax.div(total + 1, 2)

    count = lax.fori_loop(0, slots, tile_plan, 0)

    @pl.when(count & 1 == 1)
    def _():
        plan[count] = slots - 1
        plan[GROUPS + count] = plan[GROUPS + count - 1]
        plan[2 * GROUPS + count] = plan[2 * GROUPS + count - 1]
        plan[3 * GROUPS + count] = 0

    plan[COUNT] = count + (count & 1)
    x, y, c = lax.shift_right_logical(region, 3), lax.shift_right_logical(region, 1) & 3, region & 1
    for b in range(32):
        core = (c + b // 16) & 1
        outer, inner = OFFSETS[(b // 4) % 4], OFFSETS[b % 4]
        plan[ORDER_A + b] = ((x + inner) & 3) * 8 + ((y + outer) & 3) * 2 + core
        plan[ORDER_B + b] = ((x + outer) & 3) * 8 + ((y + inner) & 3) * 2 + core


def taper_of(dx, dy):
    square = jnp.maximum(dx * dx + dy * dy, 1e-30)
    inverse = lax.rsqrt(square)
    z = square * inverse
    near = square * (z * (z * (-0.25 * z + 0.5) + 0.625) - 5.0 / 3.0) + 1.0
    beyond = jnp.maximum(z - 1.0, 0.0)
    twice = beyond * beyond
    value = near + (twice * twice) * (beyond * ((2.0 / 3.0) * inverse + 1.0 / 3.0))
    return jnp.where(z <= 2.0, value, 0.0)


def halves(value):
    high = value.astype(jnp.bfloat16)
    low = (value - high.astype(jnp.float32)).astype(jnp.bfloat16)
    return high, low


def taper_kernel(half, me, plan, lattice, obs_xy, *refs):
    tapers, place_x, place_y, held, sent = refs[-5:]
    count = plan[COUNT]
    middle = lax.div(count, 2)
    start, stop = ((0, middle), (middle, count))[half]
    depth = held.shape[0]

    def place(q, carry):
        tile = me[1] * OBS_SLAB - EDGE + q
        xy = obs_xy[jnp.minimum(jnp.maximum(tile, 0), obs_xy.shape[0] - 1)]
        place_x[q] = jnp.broadcast_to(xy[0:1], (OBS_TILE, OBS_TILE)).T
        place_y[q] = jnp.broadcast_to(xy[1:2], (OBS_TILE, OBS_TILE)).T
        return carry

    lax.fori_loop(0, OBS_EXT, place, 0)

    def out_copy(i):
        k = lax.rem(i, depth)
        return pltpu.make_async_copy(held.at[k], tapers.at[i], sent.at[k])

    def group(i, carry):
        @pl.when(i >= start + depth)
        def _():
            out_copy(i - depth).wait()

        slot, q0, q1, keep = plan[i], plan[GROUPS + i], plan[2 * GROUPS + i], plan[3 * GROUPS + i]
        grid_xy = lattice[plan[MINE + slot]]
        grid_x, grid_y = grid_xy[0:1], grid_xy[1:2]
        k = lax.rem(i, depth)
        for j, q in enumerate((q0, q1)):
            away = grid_x + jnp.where(keep > j, 0.0, 16.0)
            rows = pl.ds(j * OBS_TILE, OBS_TILE)
            held[k, rows] = taper_of(away - place_x[q], grid_y - place_y[q])
        out_copy(i).start()
        return carry

    lax.fori_loop(start, stop, group, 0)

    def drain(i, carry):
        out_copy(i).wait()
        return carry

    lax.fori_loop(jnp.maximum(stop - depth, start), stop, drain, 0)


def split_kernel(*refs):
    members = 256
    pieces, (obs_out, inn_out, whole, obs, inn, here, gone) = refs[: 4 * RING], refs[4 * RING :]
    loads = []
    for k, piece in enumerate(pieces):
        place = whole.at[k // (2 * RING), k % (2 * RING)]
        loads.append(pltpu.make_async_copy(piece, place, here.at[k]))
    for load in loads:
        load.start()
    for load in loads:
        load.wait()

    def stores(q):
        return (
            pltpu.make_async_copy(obs.at[q], obs_out.at[q], gone.at[0, q]),
            pltpu.make_async_copy(inn.at[q], inn_out.at[q], gone.at[1, q]),
        )

    def tile(q, carry):
        value = whole[0, :, :, q].reshape(members, OBS_TILE)
        anom = (value - jnp.mean(value, axis=0, keepdims=True)) * (1.0 / (members - 1.0))
        high, low = halves(anom.T)
        obs[q, :OBS_TILE] = high
        obs[q, OBS_TILE:] = low
        high, low = halves(whole[1, :, :, q].reshape(members, OBS_TILE))
        inn[q, :members] = high
        inn[q, members:] = low
        for store in stores(q):
            store.start()
        return carry

    lax.fori_loop(0, OBS_EXT, tile, 0)

    def drain(q, carry):
        for store in stores(q):
            store.wait()
        return carry

    lax.fori_loop(0, OBS_EXT, drain, 0)


def analysis_kernel(
    plan, recv_any, obs_any, inn_any, tapers, out,
    recv, obs, inn, anom, total, weights, held, arrived, loaded,
):
    members = 256
    slots = recv.shape[1]
    count = plan[COUNT]
    depth = held.shape[0]

    recv_copy = pltpu.make_async_copy(recv_any, recv, loaded.at[0])
    obs_copy = pltpu.make_async_copy(obs_any, obs, loaded.at[1])
    inn_copy = pltpu.make_async_copy(inn_any, inn, loaded.at[2])
    for copy in (recv_copy, obs_copy, inn_copy):
        copy.start()

    def in_copy(i):
        k = lax.rem(i, depth)
        return pltpu.make_async_copy(tapers.at[i], held.at[k], arrived.at[k])

    def first_copy(i, carry):
        in_copy(i).start()
        return carry

    lax.fori_loop(0, jnp.minimum(count, depth - 2), first_copy, 0)

    def prepare_tile(slot, carry):
        rows = jnp.concatenate([recv[plan[ORDER_A + b], slot] for b in range(32)], axis=0)
        high, low = halves(rows - jnp.mean(rows, axis=0, keepdims=True))
        anom[slot, :, :BLOCK_NODES] = high
        anom[slot, :, BLOCK_NODES:] = low
        for b in range(32):
            total[slot, 8 * b : 8 * b + 8] = recv[plan[ORDER_B + b], slot]
        return carry

    recv_copy.wait()
    lax.fori_loop(0, slots, prepare_tile, 0)
    weights[...] = jnp.zeros_like(weights)
    obs_copy.wait()
    inn_copy.wait()

    def add_group(i, k):
        slot, q0, q1 = plan[i], plan[GROUPS + i], plan[2 * GROUPS + i]
        left = jnp.concatenate([inn[q0], inn[q1]], axis=1)
        both = jnp.dot(left, weights[k], preferred_element_type=jnp.float32)
        total[slot] += (
            both[:members, :BLOCK_NODES] + both[:members, BLOCK_NODES:] + both[members:, :BLOCK_NODES]
        )

    def weigh_group(i):
        slot = plan[i]
        left = jnp.concatenate([obs[plan[GROUPS + i]], obs[plan[2 * GROUPS + i]]], axis=0)
        both = jnp.dot(left, anom[slot], preferred_element_type=jnp.float32)
        parts = []
        for j in (0, 2 * OBS_TILE):
            top, low = both[j : j + OBS_TILE], both[j + OBS_TILE : j + 2 * OBS_TILE]
            parts.append(top[:, :BLOCK_NODES] + top[:, BLOCK_NODES:] + low[:, :BLOCK_NODES])
        return halves(held[lax.rem(i, depth)] * jnp.concatenate(parts, axis=0))

    def step(n, carry):
        i = 2 * n
        for k in range(2):
            @pl.when(i + k + depth - 2 < count)
            def _(k=k):
                in_copy(i + k + depth - 2).start()

        for k in range(2):
            in_copy(i + k).wait()
        before = jnp.maximum(i - 2, 0)
        for k in range(2):
            add_group(before + k, k)
        for k in range(2):
            high, low = weigh_group(i + k)
            weights[k, :, :BLOCK_NODES] = high
            weights[k, :, BLOCK_NODES:] = low
        return carry

    lax.fori_loop(0, lax.div(count, 2), step, 0)
    for k in range(2):
        add_group(count - 2 + k, k)

    def put(slot, carry):
        for b in range(32):
            out[plan[ORDER_B + b], slot] = total[slot, 8 * b : 8 * b + 8]
        return carry

    lax.fori_loop(0, slots, put, 0)


def unpack_kernel(order, received, out):
    def copy(p, carry):
        out[order[p]] = received[p]
        return carry

    lax.fori_loop(0, received.shape[0], copy, 0, unroll=64)


VMEM = pl.BlockSpec(memory_space=pltpu.VMEM)
SMEM = pl.BlockSpec(memory_space=pltpu.SMEM)
ANY = pl.BlockSpec(memory_space=pl.ANY)


def per_device(
    prior_matrix,
    prior_at_measurements,
    scaled_residual_vector,
    lattice_coordinates,
    measurement_coordinates,
    neighbour_block_totals,
    neighbour_block_numbers,
):
    regions = lax.axis_size("region")
    slabs = lax.axis_size("slab")
    region = lax.axis_index("region")
    slab = lax.axis_index("slab")
    tiles = neighbour_block_totals.shape[0]
    slots = tiles // regions

    me = jnp.stack((region, slab))

    both = jnp.stack((prior_at_measurements, scaled_residual_vector))
    margin = EDGE * OBS_TILE
    up = [(i, i + 1) for i in range(slabs - 1)]
    low = lax.ppermute(both[:, :, -margin:], "slab", up)
    high = lax.ppermute(both[:, :, :margin], "slab", [(t, s) for s, t in up])

    index = jnp.arange(tiles, dtype=jnp.int32)
    key = neighbour_block_totals * tiles + (tiles - 1 - index)
    rank = jnp.sum((key[None, :] > key[:, None]).astype(jnp.int32), axis=1)
    row, col = rank // regions, rank % regions
    where_to = jnp.where(row % 2 == 0, col, regions - 1 - col) * slots + (slots - 1 - row)
    order = jnp.sum(jnp.where(where_to[None, :] == index[:, None], index[None, :], 0), axis=1)

    packed, plan = pl.pallas_call(
        pack_kernel,
        out_shape=(
            jax.ShapeDtypeStruct((tiles, 8, BLOCK_NODES), jnp.float32),
            jax.ShapeDtypeStruct((768,), jnp.int32),
        ),
        in_specs=[SMEM, SMEM, SMEM, SMEM, VMEM],
        out_specs=(VMEM, SMEM),
        name="pack",
    )(
        me,
        order,
        neighbour_block_totals,
        neighbour_block_numbers.T,
        prior_matrix.reshape(8, tiles, BLOCK_NODES).transpose(1, 0, 2),
    )
    received = lax.all_to_all(packed, "region", split_axis=0, concat_axis=0, tiled=True)

    wide = jnp.concatenate([low, both, high], axis=2)
    wide = wide.reshape(2, 8, OBS_EXT, OBS_TILE).transpose(0, 2, 1, 3)
    obs = jnp.concatenate(ring_pieces(wide[0], 1, 0), axis=0)
    inn = jnp.concatenate(ring_pieces(wide[1], 0, 1), axis=0)
    obs, inn = ring_pieces(obs, 0, 1), ring_pieces(inn, 1, 0)
    obs_other, inn_other = [region_shift(obs[0], 0, 0, 1)], [region_shift(inn[0], 0, 0, 1)]
    for k in range(1, RING):
        obs_other.append(region_shift(obs[k], 0, 0, 1))
        inn_other.append(region_shift(inn[k], 0, 0, 1))
    gathered = [p.reshape(RING, OBS_EXT, 8, OBS_TILE) for p in obs + obs_other + inn + inn_other]

    tapers = []
    for half in range(2):
        tapers = [
            pl.pallas_call(
                functools.partial(taper_kernel, half),
                out_shape=jax.ShapeDtypeStruct((128, 2 * OBS_TILE, BLOCK_NODES), jnp.float32),
                in_specs=[SMEM, SMEM, VMEM, VMEM] + [ANY] * len(tapers),
                out_specs=ANY,
                scratch_shapes=[
                    pltpu.VMEM((OBS_EXT, OBS_TILE, BLOCK_NODES), jnp.float32),
                    pltpu.VMEM((OBS_EXT, OBS_TILE, BLOCK_NODES), jnp.float32),
                    pltpu.VMEM((DEPTH, 2 * OBS_TILE, BLOCK_NODES), jnp.float32),
                    pltpu.SemaphoreType.DMA((DEPTH,)),
                ],
                input_output_aliases={4: 0} if tapers else {},
                cost_estimate=pl.CostEstimate(
                    flops=5 * 10**9, bytes_accessed=4 * 2**20, transcendentals=0
                ),
            )(
                me,
                plan,
                lattice_coordinates.reshape(2, tiles, BLOCK_NODES).transpose(1, 0, 2),
                measurement_coordinates.reshape(2, -1, OBS_TILE).transpose(1, 0, 2),
                *tapers,
            )
        ]

    obs_split, inn_split = pl.pallas_call(
        split_kernel,
        out_shape=(
            jax.ShapeDtypeStruct((OBS_EXT, 2 * OBS_TILE, 256), jnp.bfloat16),
            jax.ShapeDtypeStruct((OBS_EXT, 512, OBS_TILE), jnp.bfloat16),
        ),
        in_specs=[ANY] * (4 * RING),
        out_specs=(ANY, ANY),
        scratch_shapes=[
            pltpu.VMEM((2, 2 * RING, RING, OBS_EXT, 8, OBS_TILE), jnp.float32),
            pltpu.VMEM((OBS_EXT, 2 * OBS_TILE, 256), jnp.bfloat16),
            pltpu.VMEM((OBS_EXT, 512, OBS_TILE), jnp.bfloat16),
            pltpu.SemaphoreType.DMA((4 * RING,)),
            pltpu.SemaphoreType.DMA((2, OBS_EXT)),
        ],
        cost_estimate=pl.CostEstimate(flops=5 * 10**9, bytes_accessed=10 * 2**20, transcendentals=0),
        name="split",
    )(*gathered)

    analysis = pl.pallas_call(
        analysis_kernel,
        out_shape=jax.ShapeDtypeStruct((regions, slots, 8, BLOCK_NODES), jnp.float32),
        in_specs=[SMEM] + [ANY] * 4,
        out_specs=VMEM,
        scratch_shapes=[
            pltpu.VMEM((regions, slots, 8, BLOCK_NODES), jnp.float32),
            pltpu.VMEM((OBS_EXT, 2 * OBS_TILE, 256), jnp.bfloat16),
            pltpu.VMEM((OBS_EXT, 512, OBS_TILE), jnp.bfloat16),
            pltpu.VMEM((slots, 256, 2 * BLOCK_NODES), jnp.bfloat16),
            pltpu.VMEM((slots, 256, BLOCK_NODES), jnp.float32),
            pltpu.VMEM((2, 256, 2 * BLOCK_NODES), jnp.bfloat16),
            pltpu.VMEM((DEPTH, 2 * OBS_TILE, BLOCK_NODES), jnp.float32),
            pltpu.SemaphoreType.DMA((DEPTH,)),
            pltpu.SemaphoreType.DMA((3,)),
        ],
        cost_estimate=pl.CostEstimate(flops=2 * 10**10, bytes_accessed=16 * 2**20, transcendentals=0),
        name="analysis",
    )(plan, received.reshape(regions, slots, 8, BLOCK_NODES), obs_split, inn_split, tapers[0])
    returned = lax.all_to_all(
        analysis.reshape(tiles, 8, BLOCK_NODES), "region", split_axis=0, concat_axis=0, tiled=True
    )
    out = pl.pallas_call(
        unpack_kernel,
        out_shape=jax.ShapeDtypeStruct((tiles, 8, BLOCK_NODES), jnp.float32),
        in_specs=[SMEM, VMEM],
        out_specs=VMEM,
        name="unpack",
    )(order, returned)
    return out.transpose(1, 0, 2).reshape(8, tiles * BLOCK_NODES)


def solution(mesh):
    in_specs = (
        P("region", "slab"),
        P("region", "slab"),
        P("region", "slab"),
        P(None, "slab"),
        P(),
        P("slab"),
        P("slab", None),
    )

    return jax.shard_map(
        per_device, mesh=mesh, in_specs=in_specs, out_specs=P("region", "slab"), check_vma=False
    )
```
